32 devices in a mesh: groups: 2 (over x), tile: 8 (over z, y), freq: 2 (over core).
Axes of the slice: x: 2, y: 2, z: 4, core: 2. Of those that a mesh axis runs over, the one named last changes fastest.
Arguments:
- panels: bfloat16 [8, 2, 256, 384], P('freq'), may hold values from -0.3125 to 0.3125
- snapshots: bfloat16 [16, 2, 32, 256], P(('groups', 'freq')), parts along dimension 0, may hold values from -6 to 6
- wavenumbers: float32 [8, 384], P('freq'), may hold values from 0.05 to 0.5
- mode_counts: int32 [8], P('freq'), may hold values from 48 to 384, as said below
- mode_mask: int32 [8, 3, 64], P('freq'), may hold values from 0 to 1, as said below
- mode_shapes: bfloat16 [8, 2048, 384], P('freq', 'tile'), may hold values from -6 to 6
Outputs:
- surface: float32 [32, 2048], P(('groups', 'tile', 'freq')), parts along dimension 0
The draws below stay inside these ranges and needn't reach their ends.
There are 2 independent parts, one for each index of `groups`. The reference program is written for one: setup_inputs(seed, part) draws one part's arguments, and reference() takes and returns one part's arrays. A program takes and returns all parts, laid end to end along the dimension named above; an argument that names none is the same for every part. Nothing has to cross between parts.
Inputs may be any that keep to these rules, and one draw needn't show every extreme that they name: `mode_counts`: some frequency has exactly 384 modes and some exactly 48. `mode_mask`: mode block 0 is live in every depth block of every frequency.
All inputs are finite; a program needn't handle non-finite values.
Results may differ from the reference program's by a relative error of at most 0.0005.
Values may be sent and summed in bfloat16 or wider, within the bound.
No kernel may reach another device: no remote copies, remote signals or barrier semaphores. Data moves between devices by JAX's collectives and lax.ppermute only.
A program may use at most 64 MiB of HBM per device.

```python
import math
import jax
import jax.numpy as jnp
from jax import lax

M = 256
KMAX = 384
KMIN = 48
MBLK = 128
ZBLK = 32
SNAPS = 32
DEPTHS = 2048
FREQS = 8
RANGES = 16
MODE_BLOCKS = 3
DEPTH_BLOCKS = 64


def draw_mode_counts(key, part):
    key_values, key_top, key_low = jax.random.split(key, 3)
    values = jax.random.randint(key_values, (FREQS,), KMIN, KMAX + 1)
    top_slot = jax.random.randint(key_top, (), 0, FREQS)
    low_slot = (top_slot + 1 + jax.random.randint(key_low, (), 0, FREQS - 1)) % FREQS
    positions = jnp.arange(FREQS)
    values = jnp.where(positions == top_slot, KMAX, values)
    values = jnp.where(positions == low_slot, KMIN, values)
    return values.astype(jnp.int32)


def draw_mode_mask(key, part):
    random_bits = jax.random.randint(key, (FREQS, MODE_BLOCKS, DEPTH_BLOCKS), 0, 2)
    block_index = jnp.arange(MODE_BLOCKS)[None, :, None]
    return jnp.where(block_index == 0, 1, random_bits).astype(jnp.int32)


def block_levels(own_key, shape, cuts, least, largest):
    gain, own = 1.0, jax.random.fold_in(own_key, 6)
    for position, parts in cuts:
        heights = jnp.exp(jax.random.uniform(jax.random.fold_in(own, position), (parts,), jnp.float32, least / len(cuts), largest / len(cuts)))
        gain = gain * jnp.repeat(heights, shape[position] // parts).reshape([-1 if axis == position else 1 for axis in range(len(shape))])
    return gain


def gaussian(own_key, shape, scale, most, cuts=(), held_as=jnp.bfloat16):
    entries = jax.random.normal(own_key, shape, jnp.float32) * scale
    if len(cuts) > 0:
        entries = block_levels(own_key, shape, cuts, -0.22, 0.18) * entries
    return jnp.clip(entries, min=-most, max=most).astype(held_as)


def setup_inputs(seed: int = 0, part: int = 0) -> dict:
    splits = jax.random.split(jax.random.key(seed), 7)
    part_splits = jax.random.split(jax.random.fold_in(splits[6], part), 7)
    return {
        "panels": gaussian(splits[0], (FREQS, 2, M, KMAX), KMAX ** -0.5, 0.3125, ((0, 2),)),
        "snapshots": gaussian(part_splits[1], (FREQS, 2, SNAPS, M), 1.0, 6.0, ((0, 2),)),
        "wavenumbers": jnp.clip(jnp.exp(math.log(0.5) - 2.3025851 * jax.random.uniform(splits[2], (FREQS, KMAX), jnp.float32) ** block_levels(splits[2], (FREQS, KMAX), ((0, 2),), -0.2, 0.2)), 0.05, 0.5),
        "mode_counts": draw_mode_counts(jax.random.fold_in(splits[6], 71), part),
        "mode_mask": draw_mode_mask(jax.random.fold_in(splits[6], 71), part),
        "mode_shapes": gaussian(splits[5], (FREQS, DEPTHS, KMAX), 1.0, 6.0, ((0, 2), (1, 8))),
    }


range_anchor = 1000.0
range_step = 25.0


def block_power(shapes, first_depth, first_range, range_count, panels, snapshots, wavenumbers, mode_counts, mode_mask):
    depth_count = shapes.shape[1]
    modes = shapes.shape[2]
    receivers = panels.shape[2]
    snap_count = snapshots.shape[2]
    block_count = mode_mask.shape[2]
    depth_index = first_depth + jnp.arange(depth_count, dtype=jnp.int32)
    depth_onehot = ((depth_index[:, None] // ZBLK) == jnp.arange(block_count, dtype=jnp.int32)[None, :]).astype(jnp.float32)
    distances = range_anchor + range_step * (first_range + jnp.arange(range_count, dtype=jnp.int32)).astype(jnp.float32)
    mode_index = jnp.arange(modes, dtype=jnp.int32)

    def one_freq(totals, inputs):
        shape_rows, panel_pair, snap_pair, wavenumber, mode_count, live_blocks = inputs
        depth_live = jnp.dot(depth_onehot, live_blocks.astype(jnp.float32).T)
        live_modes = jnp.repeat(depth_live, MBLK, axis=1) * (mode_index < mode_count).astype(jnp.float32)[None, :]
        shaped = shape_rows.astype(jnp.float32) * live_modes
        phases = distances[:, None] * wavenumber[None, :]
        real_part = (jnp.cos(phases)[:, None, :] * shaped[None, :, :]).reshape(-1, modes)
        imag_part = (jnp.sin(phases)[:, None, :] * shaped[None, :, :]).reshape(-1, modes)
        mode_terms = jnp.concatenate([real_part, imag_part], axis=1).astype(jnp.bfloat16)
        stacked = jnp.concatenate([jnp.concatenate([panel_pair[0], -panel_pair[1]], axis=1),
                                   jnp.concatenate([panel_pair[1], panel_pair[0]], axis=1)], axis=0)
        replica = lax.dot_general(mode_terms, stacked, (((1,), (1,)), ((), ())),
                                  preferred_element_type=jnp.float32).astype(jnp.bfloat16)
        widened = replica.astype(jnp.float32)
        energy = jnp.sum(widened * widened, axis=1) / receivers + 1e-6
        probing = jnp.concatenate([jnp.concatenate([snap_pair[0], snap_pair[1]], axis=1),
                                   jnp.concatenate([-snap_pair[1], snap_pair[0]], axis=1)], axis=0)
        projected = lax.dot_general(replica, probing, (((1,), (1,)), ((), ())), preferred_element_type=jnp.float32)
        received = jnp.sum(projected * projected, axis=1) / snap_count
        bartlett = (received / (2.0 * receivers * energy)).reshape(range_count, depth_count)
        return totals + bartlett, None

    start_totals = jnp.zeros((range_count, depth_count), jnp.float32)
    totals, _ = lax.scan(one_freq, start_totals, (shapes, panels, snapshots, wavenumbers, mode_counts, mode_mask))
    return totals


def reference(panels, snapshots, wavenumbers, mode_counts, mode_mask, mode_shapes):
    def one_range(row_index):
        return block_power(mode_shapes, 0, row_index, 1, panels, snapshots, wavenumbers, mode_counts, mode_mask)[0]

    surface = lax.map(one_range, jnp.arange(RANGES, dtype=jnp.int32))
    return surface / FREQS
```

```python
import functools

import jax
import jax.numpy as jnp
from jax import lax
from jax.experimental import pallas as pl
from jax.experimental.pallas import tpu as pltpu
from jax.sharding import PartitionSpec as P

ZBLK = 32
ROWS = 16
range_anchor = 1000.0
range_step = 25.0


def dot(a, b):
    return jnp.dot(a, b, preferred_element_type=jnp.float32)


def kernel(
    counts, mask, shapes_ref, panels_ref, snaps_ref, waves_ref, out_ref, z_ref, w_ref, phi_ref, trig_ref,
    *, ranges, scale
):
    freq = pl.program_id(0)
    depths, modes = shapes_ref.shape
    blocks = mask.shape[1]
    mblk = modes // blocks
    receivers = panels_ref.shape[1]
    snap_count = snaps_ref.shape[1]
    crows = receivers + snap_count
    count = counts[freq]
    first_block = lax.axis_index("tile") * (depths // ZBLK)

    @pl.when(freq == 0)
    def _():
        out_ref[...] = jnp.zeros_like(out_ref)

    waves = waves_ref[pl.ds(freq, 1), :]
    trig_ref[0:1, :] = jnp.cos(waves * range_anchor)
    trig_ref[1:2, :] = jnp.sin(waves * range_anchor)
    trig_ref[2:3, :] = jnp.cos(waves * (range_anchor + range_step))
    trig_ref[3:4, :] = jnp.sin(waves * (range_anchor + range_step))
    trig_ref[4:5, :] = 2.0 * jnp.cos(waves * range_step)

    def run(live_blocks):
        k = live_blocks * mblk
        lane_block = lax.broadcasted_iota(jnp.int32, (1, depths), 1) // ZBLK
        phi = shapes_ref[:, :k].T
        mode = lax.broadcasted_iota(jnp.int32, (mblk, 1), 0)
        for b in range(live_blocks):
            row = jnp.zeros((1, depths), jnp.float32)
            for zb in range(depths // ZBLK):
                row = jnp.where(lane_block == zb, mask[freq, b, first_block + zb].astype(jnp.float32), row)
            live = row * (mode + b * mblk < count).astype(jnp.float32)
            phi_ref[b * mblk:(b + 1) * mblk, :] = (
                phi[b * mblk:(b + 1) * mblk].astype(jnp.float32) * live
            ).astype(jnp.bfloat16)

        pr = panels_ref[0, :, :k]
        pi = panels_ref[1, :, :k]
        sr = snaps_ref[0]
        si = snaps_ref[1]
        z_ref[0, :receivers, :k] = pr.astype(jnp.float32)
        z_ref[1, :receivers, :k] = pi.astype(jnp.float32)
        z_ref[0, receivers:, :k] = dot(sr, pr) + dot(si, pi)
        z_ref[1, receivers:, :k] = dot(sr, pi) - dot(si, pr)

        @pl.loop(0, crows // ROWS)
        def _(i):
            lo = pl.multiple_of(i * ROWS, ROWS)
            zr = z_ref[0, pl.ds(lo, ROWS), :k]
            zi = z_ref[1, pl.ds(lo, ROWS), :k]
            c0, s0 = trig_ref[0:1, :k], trig_ref[1:2, :k]
            c1, s1 = trig_ref[2:3, :k], trig_ref[3:4, :k]
            turn = trig_ref[4:5, :k]
            re0, im0 = zr * c0 - zi * s0, zr * s0 + zi * c0
            re1, im1 = zr * c1 - zi * s1, zr * s1 + zi * c1
            for r in range(ranges):
                w_ref[r, pl.ds(lo, ROWS), :k] = re0.astype(jnp.bfloat16)
                w_ref[r, pl.ds(crows + lo, ROWS), :k] = im0.astype(jnp.bfloat16)
                re0, re1 = re1, turn * re1 - re0
                im0, im1 = im1, turn * im1 - im0

        phi_k = phi_ref[:k, :]

        @pl.loop(0, ranges)
        def _(r):
            o = dot(w_ref[r, :, :k], phi_k)
            o = o * o
            energy = jnp.sum(o[:receivers], 0, keepdims=True) + jnp.sum(
                o[crows:crows + receivers], 0, keepdims=True)
            power = jnp.sum(o[receivers:crows], 0, keepdims=True) + jnp.sum(
                o[crows + receivers:], 0, keepdims=True)
            energy = energy / receivers + 1e-06
            out_ref[pl.ds(r, 1), :] += power * (scale / snap_count) / (2.0 * receivers * energy)

    for b in range(1, blocks + 1):
        low = count > (b - 1) * mblk
        cond = jnp.logical_and(low, count <= b * mblk) if b < blocks else low
        pl.when(cond)(functools.partial(run, b))


def partials(panels, snapshots, wavenumbers, mode_counts, mode_mask, mode_shapes, ranges, all_freqs):
    freqs, depths, modes = mode_shapes.shape
    receivers, snap_count = panels.shape[2], snapshots.shape[2]
    crows = receivers + snap_count
    grid_spec = pltpu.PrefetchScalarGridSpec(
        num_scalar_prefetch=2,
        grid=(freqs,),
        in_specs=[
            pl.BlockSpec((None, depths, modes), lambda f, *_: (f, 0, 0)),
            pl.BlockSpec((None, 2, receivers, modes), lambda f, *_: (f, 0, 0, 0)),
            pl.BlockSpec((None, 2, snap_count, receivers), lambda f, *_: (f, 0, 0, 0)),
            pl.BlockSpec((freqs, modes), lambda f, *_: (0, 0)),
        ],
        out_specs=pl.BlockSpec((ranges, depths), lambda f, *_: (0, 0)),
        scratch_shapes=[
            pltpu.VMEM((2, crows, modes), jnp.float32),
            pltpu.VMEM((ranges, 2 * crows, modes), jnp.bfloat16),
            pltpu.VMEM((modes, depths), jnp.bfloat16),
            pltpu.VMEM((8, modes), jnp.float32),
        ],
    )
    return pl.pallas_call(
        functools.partial(kernel, ranges=ranges, scale=1.0 / all_freqs),
        out_shape=jax.ShapeDtypeStruct((ranges, depths), jnp.float32),
        grid_spec=grid_spec,
        compiler_params=pltpu.CompilerParams(vmem_limit_bytes=48 << 20),
        name="bartlett",
    )(mode_counts, mode_mask, mode_shapes, panels, snapshots, wavenumbers)


def on_device(panels, snapshots, wavenumbers, mode_counts, mode_mask, mode_shapes):
    freq_count = lax.axis_size("freq")
    tile_count = lax.axis_size("tile")
    depths = mode_shapes.shape[1]
    part = partials(
        panels, snapshots, wavenumbers, mode_counts, mode_mask, mode_shapes,
        tile_count * freq_count, panels.shape[0] * freq_count,
    )
    got = lax.all_to_all(part, ("tile", "freq"), 0, 0, tiled=True)
    return jnp.sum(got.reshape(tile_count, freq_count, depths), axis=1).reshape(1, -1)


def solution(mesh):
    in_specs = (
        P("freq", None, None, None),
        P(("groups", "freq"), None, None, None),
        P("freq", None),
        P("freq"),
        P("freq", None, None),
        P("freq", "tile", None),
    )
    out_specs = P(("groups", "tile", "freq"), None)
    return jax.shard_map(
        on_device, mesh=mesh, in_specs=in_specs, out_specs=out_specs, check_vma=False
    )
```

```python
import functools

import jax
import jax.numpy as jnp
from jax import lax
from jax.experimental import pallas as pl
from jax.experimental.pallas import tpu as pltpu
from jax.sharding import PartitionSpec as P

ZBLK = 32
ROWS = 16
HROWS = 32
CHUNK = 16
range_anchor = 1000.0
range_step = 25.0


def dot(a, b):
    return jnp.dot(a, b, preferred_element_type=jnp.float32)


def kernel(
    counts, shapes_hbm, panels_hbm, snaps_hbm, waves_hbm, mask_hbm, out_ref,
    shapes_v, panels_v, snaps_v, waves_v, mask_v, cos_v, sin_v, row_v, col_v, live_v,
    phi_v, phib_v, gram_v, q_v, h_v, w_v, sems,
    *, ranges, scale
):
    freqs, depths, modes = shapes_v.shape
    blocks = mask_v.shape[0]
    n = modes // blocks
    receivers = panels_v.shape[2]
    snap_count = snaps_v.shape[2]
    span = min(CHUNK, ranges)
    chunks = ranges // span
    mid = span // 2 - 1 if span > 1 else 0

    small = [
        pltpu.make_async_copy(waves_hbm, waves_v, sems.at[3, 0]),
        pltpu.make_async_copy(mask_hbm, mask_v, sems.at[4, 0]),
    ]

    def loads(f):
        return [
            pltpu.make_async_copy(panels_hbm.at[f], panels_v.at[f], sems.at[0, f]),
            pltpu.make_async_copy(shapes_hbm.at[f], shapes_v.at[f], sems.at[1, f]),
            pltpu.make_async_copy(snaps_hbm.at[f], snaps_v.at[f], sems.at[2, f]),
        ]

    for copy in small:
        copy.start()
    for f in range(freqs):
        for copy in loads(f):
            copy.start()
    for copy in small:
        copy.wait()

    out_ref[...] = jnp.zeros_like(out_ref)
    waves = waves_v[...]
    angles = jnp.concatenate(
        [waves * range_step]
        + [waves * (range_anchor + range_step * (span * c + mid)) for c in range(chunks)], axis=0)
    cos_v[...] = jnp.cos(angles)
    sin_v[...] = jnp.sin(angles)
    first_block = lax.axis_index("tile") * (depths // ZBLK)
    total_blocks = mask_v.shape[2]
    pick = (
        lax.broadcasted_iota(jnp.int32, (total_blocks, depths), 0)
        == first_block + lax.broadcasted_iota(jnp.int32, (total_blocks, depths), 1) // ZBLK
    ).astype(jnp.bfloat16)
    for b in range(blocks):
        live_v[b] = dot(mask_v[b].astype(jnp.bfloat16), pick)

    def run(freq, count, nb):
        k = nb * n
        panel_re, panel_im = panels_v.at[freq, 0], panels_v.at[freq, 1]
        pairs = [(j, (j + 1) % nb if s else j) for j in range(nb) for s in range(2)]
        if nb == 1:
            pairs = [(0, 0)]
        elif nb == 2:
            pairs = [(0, 0), (0, 1), (1, 1)]
        width = [n * sum(1 for p in pairs if p[0] == j) for j in range(nb)]

        mode = lax.broadcasted_iota(jnp.int32, (n, 1), 0)
        for b in range(nb):
            part = shapes_v[freq, :, b * n:(b + 1) * n].T.astype(jnp.float32)
            part = part * live_v[b, pl.ds(freq, 1), :]
            part = jnp.where(mode + b * n < count, part, 0.0)
            phi_v[b * n:(b + 1) * n, :] = part
            phib_v[b * n:(b + 1) * n, :] = part.astype(jnp.bfloat16)
            if nb == 3 and b == 0:
                phib_v[3 * n:, :] = part.astype(jnp.bfloat16)

        snaps = jnp.concatenate([snaps_v[freq, 0], snaps_v[freq, 1]], axis=0)
        sp_re = dot(snaps, panel_re[:, :k])
        sp_im = dot(snaps, panel_im[:, :k])
        q_v[0, :, :k] = sp_re[:snap_count] + sp_im[snap_count:]
        q_v[1, :, :k] = sp_im[:snap_count] - sp_re[snap_count:]
        wide = snaps.astype(jnp.float32)
        snap_energy = jnp.maximum(jnp.sum(wide * wide, keepdims=True), 1e-30)

        diag = []
        eye = lax.broadcasted_iota(jnp.int32, (n, n), 0) == lax.broadcasted_iota(jnp.int32, (n, n), 1)
        for p, (j, q) in enumerate(pairs):
            left_re = panel_re[:, j * n:(j + 1) * n].T
            left_im = panel_im[:, j * n:(j + 1) * n].T
            right_re = panel_re[:, q * n:(q + 1) * n]
            right_im = panel_im[:, q * n:(q + 1) * n]
            one = dot(left_re, jnp.concatenate([right_re, right_im], axis=1))
            two = dot(left_im, jnp.concatenate([right_im, right_re], axis=1))
            g_re = one[:, :n] + two[:, :n]
            g_im = one[:, n:] - two[:, n:]
            if j == q:
                diag.append(jnp.sum(jnp.where(eye, g_re, 0.0), axis=1, keepdims=True))
                g_re = jnp.where(eye, 0.0, g_re)
                g_im = jnp.where(eye, 0.0, g_im)
            else:
                g_re, g_im = g_re * 2.0, g_im * 2.0
            gram_v[p, 0] = g_re
            gram_v[p, 1] = g_im
        level = jnp.zeros((1, depths), jnp.float32)
        for j in range(nb):
            part = phi_v[j * n:(j + 1) * n, :]
            level += jnp.sum(part * part * diag[j], axis=0, keepdims=True)

        for c in range(chunks):
            base = (c + 1) * freqs + freq
            cs, ss = cos_v[pl.ds(freq, 1), :], sin_v[pl.ds(freq, 1), :]
            c0, s0 = cos_v[pl.ds(base, 1), :], sin_v[pl.ds(base, 1), :]
            rows = [c0, s0, c0 * cs - s0 * ss, s0 * cs + c0 * ss, cs, ss, cs, ss]
            for i, row in enumerate(rows):
                row_v[i:i + 1, :] = row
            col_v[...] = row_v[...].T

            @pl.loop(0, snap_count // ROWS)
            def _(i):
                lo = pl.multiple_of(i * ROWS, ROWS)
                zr, zi = q_v[0, pl.ds(lo, ROWS), :k], q_v[1, pl.ds(lo, ROWS), :k]
                c0, s0 = row_v[0:1, :k], row_v[1:2, :k]
                c1, s1 = row_v[2:3, :k], row_v[3:4, :k]
                turn = 2.0 * row_v[4:5, :k]
                re0, im0 = zr * c0 - zi * s0, zr * s0 + zi * c0
                re1, im1 = zr * c1 - zi * s1, zr * s1 + zi * c1
                for step in (1, -1):
                    a = (re0, im0), (re1, im1)
                    if step < 0:
                        a = (turn * re0 - re1, turn * im0 - im1), (re0, im0)
                    for r in range(mid, span) if step > 0 else range(mid - 1, -1, -1):
                        at = r * 2 * snap_count
                        w_v[pl.ds(at + lo, ROWS), :k] = a[0][0].astype(jnp.bfloat16)
                        w_v[pl.ds(at + snap_count + lo, ROWS), :k] = a[0][1].astype(jnp.bfloat16)
                        if step > 0:
                            a = a[1], tuple(turn * x - y for x, y in zip(a[1], a[0]))
                        else:
                            a = tuple(turn * x - y for x, y in zip(a[0], a[1])), a[0]

            for p, (j, q) in enumerate(pairs):
                slot = n * (p - [x[0] for x in pairs].index(j))
                at = slice(q * n, (q + 1) * n)

                def form(lo):
                    g_re, g_im = gram_v[p, 0, pl.ds(lo, HROWS), :], gram_v[p, 1, pl.ds(lo, HROWS), :]
                    col = col_v[pl.ds(j * n + lo, HROWS), :]

                    def turned(x):
                        ck, sk = row_v[x:x + 1, at], row_v[x + 1:x + 2, at]
                        return (g_re * ck - g_im * sk) * col[:, x:x + 1] + (
                            g_re * sk + g_im * ck) * col[:, x + 1:x + 2]

                    low, high = turned(0), turned(2)
                    turn = 2.0 * (row_v[4:5, at] * col[:, 4:5] + row_v[5:6, at] * col[:, 5:6])
                    h0, h1 = low, high
                    for r in range(mid, span):
                        h_v[j, pl.ds(r * n + lo, HROWS), slot:slot + n] = h0.astype(jnp.bfloat16)
                        if r + 1 < span:
                            h0, h1 = h1, turn * h1 - h0
                    h0, h1 = turn * low - high, low
                    for r in range(mid - 1, -1, -1):
                        h_v[j, pl.ds(r * n + lo, HROWS), slot:slot + n] = h0.astype(jnp.bfloat16)
                        if r:
                            h0, h1 = turn * h0 - h1, h0

                for i in range(n // HROWS):
                    form(i * HROWS)

            y = dot(w_v[:, :k], phib_v[:k, :])
            power = jnp.sum(jnp.sum((y * y).reshape(span, -1, 8, depths), axis=1), axis=1)
            energy = 0.0
            for j in range(nb):
                y = dot(h_v[j, :, :width[j]], phib_v[j * n:j * n + width[j], :])
                y = y.reshape(span, n, depths) * phi_v[j * n:(j + 1) * n, :][None]
                energy = energy + jnp.sum(y.reshape(span, n // 8, 8, depths), axis=1)
            energy = level + jnp.sum(energy, axis=1)
            energy = jnp.maximum(energy, power / snap_energy)
            energy = energy / receivers + 1e-06
            out_ref[c * span:(c + 1) * span, :] += power * (scale / snap_count) / (
                2.0 * receivers * energy)

    @pl.loop(0, freqs)
    def _(freq):
        for copy in loads(freq):
            copy.wait()
        count = counts[freq]
        for b in range(1, blocks + 1):
            low = count > (b - 1) * n
            cond = jnp.logical_and(low, count <= b * n) if b < blocks else low
            pl.when(cond)(functools.partial(run, freq, count, b))


def partials(panels, snapshots, wavenumbers, mode_counts, mode_mask, mode_shapes, ranges, all_freqs):
    freqs, depths, modes = mode_shapes.shape
    receivers, snap_count = panels.shape[2], snapshots.shape[2]
    blocks, total_blocks = mode_mask.shape[1], mode_mask.shape[2]
    n = modes // blocks
    span = min(CHUNK, ranges)
    trig_rows = freqs * (ranges // span + 1)
    hbm = pl.BlockSpec(memory_space=pltpu.HBM)
    f32, bf16 = jnp.float32, jnp.bfloat16
    return pl.pallas_call(
        functools.partial(kernel, ranges=ranges, scale=1.0 / all_freqs),
        out_shape=jax.ShapeDtypeStruct((ranges, depths), f32),
        in_specs=[pl.BlockSpec(memory_space=pltpu.SMEM)] + [hbm] * 5,
        out_specs=pl.BlockSpec(memory_space=pltpu.VMEM),
        scratch_shapes=[
            pltpu.VMEM((freqs, depths, modes), bf16),
            pltpu.VMEM((freqs, 2, receivers, modes), bf16),
            pltpu.VMEM((freqs, 2, snap_count, receivers), bf16),
            pltpu.VMEM((freqs, modes), f32),
            pltpu.VMEM((blocks, freqs, total_blocks), jnp.int32),
            pltpu.VMEM((trig_rows, modes), f32),
            pltpu.VMEM((trig_rows, modes), f32),
            pltpu.VMEM((8, modes), f32),
            pltpu.VMEM((modes, 8), f32),
            pltpu.VMEM((blocks, freqs, depths), f32),
            pltpu.VMEM((modes, depths), f32),
            pltpu.VMEM((modes + n, depths), bf16),
            pltpu.VMEM((2 * blocks, 2, n, n), f32),
            pltpu.VMEM((2, snap_count, modes), f32),
            pltpu.VMEM((blocks, span * n, 2 * n), bf16),
            pltpu.VMEM((span * 2 * snap_count, modes), bf16),
            pltpu.SemaphoreType.DMA((5, freqs)),
        ],
        compiler_params=pltpu.CompilerParams(vmem_limit_bytes=56 << 20),
        name="bartlett",
    )(mode_counts, mode_shapes, panels, snapshots, wavenumbers, jnp.transpose(mode_mask, (1, 0, 2)))


def on_device(panels, snapshots, wavenumbers, mode_counts, mode_mask, mode_shapes):
    freq_count = lax.axis_size("freq")
    tile_count = lax.axis_size("tile")
    depths = mode_shapes.shape[1]
    part = partials(
        panels, snapshots, wavenumbers, mode_counts, mode_mask, mode_shapes,
        tile_count * freq_count, panels.shape[0] * freq_count,
    )
    got = lax.all_to_all(part, ("tile", "freq"), 0, 0, tiled=True)
    return jnp.sum(got.reshape(tile_count, freq_count, depths), axis=1).reshape(1, -1)


def solution(mesh):
    in_specs = (
        P("freq", None, None, None),
        P(("groups", "freq"), None, None, None),
        P("freq", None),
        P("freq"),
        P("freq", None, None),
        P("freq", "tile", None),
    )
    out_specs = P(("groups", "tile", "freq"), None)
    return jax.shard_map(
        on_device, mesh=mesh, in_specs=in_specs, out_specs=out_specs, check_vma=False
    )
```

```python
import functools

import jax
import jax.numpy as jnp
from jax import lax
from jax.experimental import pallas as pl
from jax.experimental.pallas import tpu as pltpu
from jax.sharding import PartitionSpec as P

ZBLK = 32
ROWS = 16
HROWS = 32
PARTS = 4
CHUNK = 16
range_anchor = 1000.0
range_step = 25.0


def dot(a, b):
    return jnp.dot(a, b, preferred_element_type=jnp.float32)


def kernel(
    counts, shapes_hbm, panels_hbm, snaps_hbm, waves_hbm, mask_hbm, out_ref,
    shapes_v, panels_v, snaps_v, waves_v, mask_v, cos_v, sin_v, row_v, col_v, live_v,
    phi_v, phib_v, gram_v, q_v, h_v, w_v, level_v, energy_v, power_v, sum_v, sems,
    *, ranges, scale
):
    freqs, depths, modes = shapes_v.shape
    blocks = mask_v.shape[0]
    n = modes // blocks
    receivers = panels_v.shape[2]
    snap_count = snaps_v.shape[2]
    span = min(CHUNK, ranges)
    chunks = ranges // span
    mid = span // 2 - 1 if span > 1 else 0

    small = [
        pltpu.make_async_copy(waves_hbm, waves_v, sems.at[3, 0]),
        pltpu.make_async_copy(mask_hbm, mask_v, sems.at[4, 0]),
    ]

    def loads(f):
        return [
            pltpu.make_async_copy(panels_hbm.at[f], panels_v.at[f], sems.at[0, f]),
            pltpu.make_async_copy(shapes_hbm.at[f], shapes_v.at[f], sems.at[1, f]),
            pltpu.make_async_copy(snaps_hbm.at[f], snaps_v.at[f], sems.at[2, f]),
        ]

    for copy in small:
        copy.start()
    for f in range(freqs):
        for copy in loads(f):
            copy.start()
    for copy in small:
        copy.wait()

    sum_v[...] = jnp.zeros_like(sum_v)
    waves = waves_v[...]
    angles = jnp.concatenate(
        [waves * range_step]
        + [waves * (range_anchor + range_step * (span * c + mid)) for c in range(chunks)], axis=0)
    cos_v[...] = jnp.cos(angles)
    sin_v[...] = jnp.sin(angles)
    first_block = lax.axis_index("tile") * (depths // ZBLK)
    total_blocks = mask_v.shape[2]
    pick = (
        lax.broadcasted_iota(jnp.int32, (total_blocks, depths), 0)
        == first_block + lax.broadcasted_iota(jnp.int32, (total_blocks, depths), 1) // ZBLK
    ).astype(jnp.bfloat16)
    for b in range(blocks):
        live_v[b] = dot(mask_v[b].astype(jnp.bfloat16), pick)

    def run(freq, count, nb):
        k = nb * n
        panel_re, panel_im = panels_v.at[freq, 0], panels_v.at[freq, 1]
        pairs = [(j, (j + 1) % nb if s else j) for j in range(nb) for s in range(2)]
        if nb == 1:
            pairs = [(0, 0)]
        elif nb == 2:
            pairs = [(0, 0), (0, 1), (1, 1)]
        width = [n * sum(1 for p in pairs if p[0] == j) for j in range(nb)]

        mode = lax.broadcasted_iota(jnp.int32, (n, 1), 0)
        for b in range(nb):
            part = shapes_v[freq, :, b * n:(b + 1) * n].T.astype(jnp.float32)
            part = part * live_v[b, pl.ds(freq, 1), :]
            part = jnp.where(mode + b * n < count, part, 0.0)
            phi_v[b * n:(b + 1) * n, :] = part
            phib_v[b * n:(b + 1) * n, :] = part.astype(jnp.bfloat16)
            if nb == 3 and b == 0:
                phib_v[3 * n:, :] = part.astype(jnp.bfloat16)

        snaps = jnp.concatenate([snaps_v[freq, 0], snaps_v[freq, 1]], axis=0)
        sp_re = dot(snaps, panel_re[:, :k])
        sp_im = dot(snaps, panel_im[:, :k])
        q_v[0, :, :k] = sp_re[:snap_count] + sp_im[snap_count:]
        q_v[1, :, :k] = sp_im[:snap_count] - sp_re[snap_count:]
        wide = snaps.astype(jnp.float32)
        snap_energy = jnp.maximum(jnp.sum(wide * wide, keepdims=True), 1e-30)

        eye = lax.broadcasted_iota(jnp.int32, (n, n), 0) == lax.broadcasted_iota(jnp.int32, (n, n), 1)

        def gram(p):
            j, q = pairs[p]
            left_re = panel_re[:, j * n:(j + 1) * n].T
            left_im = panel_im[:, j * n:(j + 1) * n].T
            right_re = panel_re[:, q * n:(q + 1) * n]
            right_im = panel_im[:, q * n:(q + 1) * n]
            one = dot(left_re, jnp.concatenate([right_re, right_im], axis=1))
            two = dot(left_im, jnp.concatenate([right_im, right_re], axis=1))
            g_re = one[:, :n] + two[:, :n]
            g_im = one[:, n:] - two[:, n:]
            if j == q:
                diag = jnp.sum(jnp.where(eye, g_re, 0.0), axis=1, keepdims=True)
                part = phi_v[j * n:(j + 1) * n, :]
                level_v[j:j + 1, :] = jnp.sum(part * part * diag, axis=0, keepdims=True)
                g_re = jnp.where(eye, 0.0, g_re)
                g_im = jnp.where(eye, 0.0, g_im)
            else:
                g_re, g_im = g_re * 2.0, g_im * 2.0
            gram_v[p, 0] = g_re
            gram_v[p, 1] = g_im

        def form_q(b):
            at = slice(b * n, (b + 1) * n)
            zr, zi = q_v[0, :, at], q_v[1, :, at]
            c0, s0 = row_v[0:1, at], row_v[1:2, at]
            c1, s1 = row_v[2:3, at], row_v[3:4, at]
            turn = jnp.broadcast_to(2.0 * row_v[4:5, at], zr.shape)
            for row, low, high in (
                (0, zr * c0 - zi * s0, zr * c1 - zi * s1),
                (snap_count, zr * s0 + zi * c0, zr * s1 + zi * c1),
            ):
                a, z = low, high
                for r in range(mid, span):
                    lo = r * 2 * snap_count + row
                    w_v[lo:lo + snap_count, at] = a.astype(jnp.bfloat16)
                    if r + 1 < span:
                        a, z = z, turn * z - a
                a, z = turn * low - high, low
                for r in range(mid - 1, -1, -1):
                    lo = r * 2 * snap_count + row
                    w_v[lo:lo + snap_count, at] = a.astype(jnp.bfloat16)
                    if r:
                        a, z = turn * a - z, a

        def form_h(p, lo):
            j, q = pairs[p]
            slot = n * (p - [x[0] for x in pairs].index(j))
            at = slice(q * n, (q + 1) * n)
            g_re, g_im = gram_v[p, 0, lo:lo + HROWS, :], gram_v[p, 1, lo:lo + HROWS, :]
            col = col_v[j * n + lo:j * n + lo + HROWS, :]

            def turned(x):
                ck, sk = row_v[x:x + 1, at], row_v[x + 1:x + 2, at]
                return (g_re * ck - g_im * sk) * col[:, x:x + 1] + (
                    g_re * sk + g_im * ck) * col[:, x + 1:x + 2]

            low, high = turned(0), turned(2)
            turn = 2.0 * (row_v[4:5, at] * col[:, 4:5] + row_v[5:6, at] * col[:, 5:6])
            h0, h1 = low, high
            for r in range(mid, span):
                h_v[j, r * n + lo:r * n + lo + HROWS, slot:slot + n] = h0.astype(jnp.bfloat16)
                if r + 1 < span:
                    h0, h1 = h1, turn * h1 - h0
            h0, h1 = turn * low - high, low
            for r in range(mid - 1, -1, -1):
                h_v[j, r * n + lo:r * n + lo + HROWS, slot:slot + n] = h0.astype(jnp.bfloat16)
                if r:
                    h0, h1 = turn * h0 - h1, h0

        step = span // PARTS if span % PARTS == 0 else span

        def power_of(c):
            y = dot(w_v[2 * snap_count * c:2 * snap_count * (c + step), :k], phib_v[:k, :])
            power_v[c:c + step] = jnp.sum((y * y).reshape(step, -1, 8, depths), axis=1)

        def energy_of(j, c):
            y = dot(h_v[j, n * c:n * (c + step), :width[j]], phib_v[j * n:j * n + width[j], :])
            y = y.reshape(step, n, depths) * phi_v[j * n:(j + 1) * n, :][None]
            y = jnp.sum(y.reshape(step, n // 8, 8, depths), axis=1)
            energy_v[c:c + step] = y if j == 0 else energy_v[c:c + step] + y

        def both(one, two):
            done = 0
            for i, task in enumerate(one):
                task()
                upto = (i + 1) * len(two) // len(one)
                for other in two[done:upto]:
                    other()
                done = upto
            for other in two[done:]:
                other()

        of = [[p for p in range(len(pairs)) if pairs[p][0] == j] for j in range(nb)]
        bind = functools.partial
        forms = [[bind(form_h, p, lo) for lo in range(0, n, HROWS) for p in of[j]] for j in range(nb)]
        grams = [[bind(gram, p) for p in of[j]] for j in range(nb)]
        starts = range(0, span, step)
        energies = [[bind(energy_of, j, c) for c in starts] for j in range(nb)]
        powers = [bind(power_of, c) for c in starts]

        for c in range(chunks):
            base = (c + 1) * freqs + freq
            cs, ss = cos_v[pl.ds(freq, 1), :], sin_v[pl.ds(freq, 1), :]
            c0, s0 = cos_v[pl.ds(base, 1), :], sin_v[pl.ds(base, 1), :]
            rows = [c0, s0, c0 * cs - s0 * ss, s0 * cs + c0 * ss, cs, ss, cs, ss]
            for i, row in enumerate(rows):
                row_v[i:i + 1, :] = row
            col_v[...] = row_v[...].T

            first = c == 0
            if first:
                for task in grams[0]:
                    task()
            both([bind(form_q, b) for b in range(nb)], grams[1] if first and nb > 1 else [])
            both(forms[0], (grams[2] if first and nb > 2 else []) + powers)
            for j in range(1, nb):
                both(forms[j], energies[j - 1])
            for task in energies[nb - 1]:
                task()
            power = jnp.sum(power_v[...], axis=1)
            energy = jnp.sum(level_v[:nb], axis=0, keepdims=True) + jnp.sum(energy_v[...], axis=1)
            energy = jnp.maximum(energy, power / snap_energy)
            energy = energy / receivers + 1e-06
            sum_v[c * span:(c + 1) * span, :] += power * (scale / snap_count) / (
                2.0 * receivers * energy)

    @pl.loop(0, freqs)
    def _(freq):
        for copy in loads(freq):
            copy.wait()
        count = counts[freq]
        for b in range(1, blocks + 1):
            low = count > (b - 1) * n
            cond = jnp.logical_and(low, count <= b * n) if b < blocks else low
            pl.when(cond)(functools.partial(run, freq, count, b))

    for r in range(ranges):
        out_ref[r] = sum_v[r:r + 1, :]


def partials(panels, snapshots, wavenumbers, mode_counts, mode_mask, mode_shapes, ranges, all_freqs):
    freqs, depths, modes = mode_shapes.shape
    receivers, snap_count = panels.shape[2], snapshots.shape[2]
    blocks, total_blocks = mode_mask.shape[1], mode_mask.shape[2]
    n = modes // blocks
    span = min(CHUNK, ranges)
    trig_rows = freqs * (ranges // span + 1)
    hbm = pl.BlockSpec(memory_space=pltpu.HBM)
    f32, bf16 = jnp.float32, jnp.bfloat16
    return pl.pallas_call(
        functools.partial(kernel, ranges=ranges, scale=1.0 / all_freqs),
        out_shape=jax.ShapeDtypeStruct((ranges, 1, depths), f32),
        in_specs=[pl.BlockSpec(memory_space=pltpu.SMEM)] + [hbm] * 5,
        out_specs=pl.BlockSpec(memory_space=pltpu.VMEM),
        scratch_shapes=[
            pltpu.VMEM((freqs, depths, modes), bf16),
            pltpu.VMEM((freqs, 2, receivers, modes), bf16),
            pltpu.VMEM((freqs, 2, snap_count, receivers), bf16),
            pltpu.VMEM((freqs, modes), f32),
            pltpu.VMEM((blocks, freqs, total_blocks), jnp.int32),
            pltpu.VMEM((trig_rows, modes), f32),
            pltpu.VMEM((trig_rows, modes), f32),
            pltpu.VMEM((8, modes), f32),
            pltpu.VMEM((modes, 8), f32),
            pltpu.VMEM((blocks, freqs, depths), f32),
            pltpu.VMEM((modes, depths), f32),
            pltpu.VMEM((modes + n, depths), bf16),
            pltpu.VMEM((2 * blocks, 2, n, n), f32),
            pltpu.VMEM((2, snap_count, modes), f32),
            pltpu.VMEM((blocks, span * n, 2 * n), bf16),
            pltpu.VMEM((span * 2 * snap_count, modes), bf16),
            pltpu.VMEM((8, depths), f32),
            pltpu.VMEM((span, 8, depths), f32),
            pltpu.VMEM((span, 8, depths), f32),
            pltpu.VMEM((ranges, depths), f32),
            pltpu.SemaphoreType.DMA((5, freqs)),
        ],
        compiler_params=pltpu.CompilerParams(vmem_limit_bytes=56 << 20),
        name="bartlett",
    )(mode_counts, mode_shapes, panels, snapshots, wavenumbers, jnp.transpose(mode_mask, (1, 0, 2)))


def on_device(panels, snapshots, wavenumbers, mode_counts, mode_mask, mode_shapes):
    freq_count = lax.axis_size("freq")
    tile_count = lax.axis_size("tile")
    depths = mode_shapes.shape[1]
    part = partials(
        panels, snapshots, wavenumbers, mode_counts, mode_mask, mode_shapes,
        tile_count * freq_count, panels.shape[0] * freq_count,
    )
    got = lax.all_to_all(part, ("tile", "freq"), 0, 0, tiled=True)
    return jnp.sum(got.reshape(tile_count, freq_count, depths), axis=1).reshape(1, -1)


def solution(mesh):
    in_specs = (
        P("freq", None, None, None),
        P(("groups", "freq"), None, None, None),
        P("freq", None),
        P("freq"),
        P("freq", None, None),
        P("freq", "tile", None),
    )
    out_specs = P(("groups", "tile", "freq"), None)
    return jax.shard_map(
        on_device, mesh=mesh, in_specs=in_specs, out_specs=out_specs, check_vma=False
    )
```

```python
import functools

import jax
import jax.numpy as jnp
from jax import lax
from jax.experimental import pallas as pl
from jax.experimental.pallas import tpu as pltpu
from jax.sharding import PartitionSpec as P

ZBLK = 32
ROWS = 16
HROWS = 32
PARTS = 4
CHUNK = 16
range_anchor = 1000.0
range_step = 25.0


def dot(a, b):
    return jnp.dot(a, b, preferred_element_type=jnp.float32)


def pieces(x):
    hi = x.astype(jnp.bfloat16).astype(jnp.float32)
    mid = (x - hi).astype(jnp.bfloat16).astype(jnp.float32)
    return hi, mid, x - hi - mid


def kernel(
    counts_hbm, shapes_hbm, panels_hbm, snaps_hbm, waves_hbm, mask_hbm, out_ref,
    counts, shapes_v, panels_v, snaps_v, waves_v, mask_v, cos_v, sin_v, row_v, col_v, live_v,
    phi_v, phib_v, gram_v, q_v, h0_v, h1_v, h2_v, w_v, level_v, energy_v, power_v, sum_v, pair_v, turn_v, sems,
    *, ranges, scale
):
    h_v = (h0_v, h1_v, h2_v)
    freqs, depths, modes = shapes_v.shape
    blocks = mask_v.shape[0]
    n = modes // blocks
    receivers = panels_v.shape[2]
    snap_count = snaps_v.shape[2]
    span = min(CHUNK, ranges)
    chunks = ranges // span
    mid = span // 2 - 1 if span > 1 else 0

    small = [
        pltpu.make_async_copy(waves_hbm, waves_v, sems.at[3, 0]),
        pltpu.make_async_copy(mask_hbm, mask_v, sems.at[4, 0]),
        pltpu.make_async_copy(counts_hbm, counts, sems.at[4, 1]),
    ]

    def loads(f):
        return [
            pltpu.make_async_copy(panels_hbm.at[f], panels_v.at[f], sems.at[0, f]),
            pltpu.make_async_copy(shapes_hbm.at[f], shapes_v.at[f], sems.at[1, f]),
            pltpu.make_async_copy(snaps_hbm.at[f], snaps_v.at[f], sems.at[2, f]),
        ]

    for copy in small:
        copy.start()
    for f in range(freqs):
        for copy in loads(f):
            copy.start()
    for copy in small:
        copy.wait()

    sum_v[...] = jnp.zeros_like(sum_v)
    waves = waves_v[...]
    angles = jnp.concatenate(
        [waves * range_step]
        + [waves * (range_anchor + range_step * (span * c + mid)) for c in range(chunks)], axis=0)
    cos_v[...] = jnp.cos(angles)
    sin_v[...] = jnp.sin(angles)
    first_block = lax.axis_index("tile") * (depths // ZBLK)
    total_blocks = mask_v.shape[2]
    pick = (
        lax.broadcasted_iota(jnp.int32, (total_blocks, depths), 0)
        == first_block + lax.broadcasted_iota(jnp.int32, (total_blocks, depths), 1) // ZBLK
    ).astype(jnp.bfloat16)
    for b in range(blocks):
        live_v[b] = dot(mask_v[b].astype(jnp.bfloat16), pick)

    def run(freq, count, nb):
        k = nb * n
        panel_re, panel_im = panels_v.at[freq, 0], panels_v.at[freq, 1]
        pairs = [(j, (j + 1) % nb if s else j) for j in range(nb) for s in range(2)]
        if nb == 1:
            pairs = [(0, 0)]
        elif nb == 2:
            pairs = [(0, 0), (0, 1), (1, 1)]
        width = [n * sum(1 for p in pairs if p[0] == j) for j in range(nb)]

        mode = lax.broadcasted_iota(jnp.int32, (n, 1), 0)
        for b in range(nb):
            part = shapes_v[freq, :, b * n:(b + 1) * n].T.astype(jnp.float32)
            part = part * live_v[b, pl.ds(freq, 1), :]
            part = jnp.where(mode + b * n < count, part, 0.0)
            phi_v[b * n:(b + 1) * n, :] = part
            phib_v[b * n:(b + 1) * n, :] = part.astype(jnp.bfloat16)
            if nb == 3 and b == 0:
                phib_v[3 * n:, :] = part.astype(jnp.bfloat16)

        snaps = jnp.concatenate([snaps_v[freq, 0], snaps_v[freq, 1]], axis=0)
        sp_re = dot(snaps, panel_re[:, :k])
        sp_im = dot(snaps, panel_im[:, :k])
        q_v[0, :, :k] = sp_re[:snap_count] + sp_im[snap_count:]
        q_v[1, :, :k] = sp_im[:snap_count] - sp_re[snap_count:]
        wide = snaps.astype(jnp.float32)
        snap_energy = jnp.maximum(jnp.sum(wide * wide, keepdims=True), 1e-30)

        eye = lax.broadcasted_iota(jnp.int32, (n, n), 0) == lax.broadcasted_iota(jnp.int32, (n, n), 1)

        def gram(p):
            j, q = pairs[p]
            left_re = panel_re[:, j * n:(j + 1) * n].T
            left_im = panel_im[:, j * n:(j + 1) * n].T
            right_re = panel_re[:, q * n:(q + 1) * n]
            right_im = panel_im[:, q * n:(q + 1) * n]
            one = dot(left_re, jnp.concatenate([right_re, right_im], axis=1))
            two = dot(left_im, jnp.concatenate([right_im, right_re], axis=1))
            g_re = one[:, :n] + two[:, :n]
            g_im = one[:, n:] - two[:, n:]
            if j == q:
                diag = jnp.sum(jnp.where(eye, g_re, 0.0), axis=1, keepdims=True)
                part = phi_v[j * n:(j + 1) * n, :]
                level_v[j:j + 1, :] = jnp.sum(part * part * diag, axis=0, keepdims=True)
                g_re = jnp.where(eye, 0.0, g_re)
                g_im = jnp.where(eye, 0.0, g_im)
            else:
                g_re, g_im = g_re * 2.0, g_im * 2.0
            gram_v[p, 0] = g_re
            gram_v[p, 1] = g_im

        def turns():
            for p, (j, q) in enumerate(pairs):
                right = jnp.concatenate([pair_v[x, :, q * n:(q + 1) * n] for x in range(5)], axis=1)
                both_of = dot(col_v[j * n:(j + 1) * n, :], right)
                for x in range(5):
                    turn_v[p, x] = both_of[:, x * n:(x + 1) * n]

        def form_q(b):
            at = slice(b * n, (b + 1) * n)
            zr, zi = q_v[0, :, at], q_v[1, :, at]
            c0, s0 = row_v[0:1, at], row_v[1:2, at]
            c1, s1 = row_v[2:3, at], row_v[3:4, at]
            turn = jnp.broadcast_to(2.0 * row_v[4:5, at], zr.shape)
            for row, low, high in (
                (0, zr * c0 - zi * s0, zr * c1 - zi * s1),
                (snap_count, zr * s0 + zi * c0, zr * s1 + zi * c1),
            ):
                a, z = low, high
                for r in range(mid, span):
                    lo = r * 2 * snap_count + row
                    w_v[lo:lo + snap_count, at] = a.astype(jnp.bfloat16)
                    if r + 1 < span:
                        a, z = z, turn * z - a
                a, z = turn * low - high, low
                for r in range(mid - 1, -1, -1):
                    lo = r * 2 * snap_count + row
                    w_v[lo:lo + snap_count, at] = a.astype(jnp.bfloat16)
                    if r:
                        a, z = turn * a - z, a

        def form_h(p, lo):
            j, q = pairs[p]
            slot = n * (p - [x[0] for x in pairs].index(j))
            g_re, g_im = gram_v[p, 0, lo:lo + HROWS, :], gram_v[p, 1, lo:lo + HROWS, :]

            cos0, sin0, cos1, sin1, turn = (
                turn_v[p, x, lo:lo + HROWS, :] for x in range(5))
            low, high = g_re * cos0 - g_im * sin0, g_re * cos1 - g_im * sin1
            h0, h1 = low, high
            for r in range(mid, span):
                h_v[j][r * n + lo:r * n + lo + HROWS, slot:slot + n] = h0.astype(jnp.bfloat16)
                if r + 1 < span:
                    h0, h1 = h1, turn * h1 - h0
            h0, h1 = turn * low - high, low
            for r in range(mid - 1, -1, -1):
                h_v[j][r * n + lo:r * n + lo + HROWS, slot:slot + n] = h0.astype(jnp.bfloat16)
                if r:
                    h0, h1 = turn * h0 - h1, h0

        step = span // PARTS if span % PARTS == 0 else span

        def power_of(c):
            y = dot(w_v[2 * snap_count * c:2 * snap_count * (c + step), :k], phib_v[:k, :])
            power_v[c:c + step] = jnp.sum((y * y).reshape(step, -1, 8, depths), axis=1)

        def energy_of(j, c):
            y = dot(h_v[j][n * c:n * (c + step), :width[j]], phib_v[j * n:j * n + width[j], :])
            y = y.reshape(step, n, depths) * phi_v[j * n:(j + 1) * n, :][None]
            y = jnp.sum(y.reshape(step, n // 8, 8, depths), axis=1)
            energy_v[c:c + step] = y if j == 0 else energy_v[c:c + step] + y

        def both(one, two):
            done = 0
            for i, task in enumerate(one):
                task()
                upto = (i + 1) * len(two) // len(one)
                for other in two[done:upto]:
                    other()
                done = upto
            for other in two[done:]:
                other()

        of = [[p for p in range(len(pairs)) if pairs[p][0] == j] for j in range(nb)]
        bind = functools.partial
        forms = [[bind(form_h, p, lo) for lo in range(0, n, HROWS) for p in of[j]] for j in range(nb)]
        grams = [[bind(gram, p) for p in of[j]] for j in range(nb)]
        starts = range(0, span, step)
        energies = [[bind(energy_of, j, c) for c in starts] for j in range(nb)]
        powers = [bind(power_of, c) for c in starts]

        for c in range(chunks):
            base = (c + 1) * freqs + freq
            cs, ss = cos_v[pl.ds(freq, 1), :], sin_v[pl.ds(freq, 1), :]
            c0, s0 = cos_v[pl.ds(base, 1), :], sin_v[pl.ds(base, 1), :]
            rows = [c0, s0, c0 * cs - s0 * ss, s0 * cs + c0 * ss, cs, ss, cs * 0.0, ss * 0.0]
            for i, row in enumerate(rows):
                row_v[i:i + 1, :] = row
            zero = jnp.zeros_like(c0)
            c1, s1 = rows[2], rows[3]
            for x, (at, one, two) in enumerate((
                (0, c0, s0), (0, s0, -c0), (2, c1, s1), (2, s1, -c1), (4, 2.0 * cs, 2.0 * ss))):
                spread = jnp.concatenate(
                    [one if i == at else two if i == at + 1 else zero for i in range(8)], axis=0)
                hi, mid_, lo = pieces(spread)
                pair_v[x] = jnp.concatenate([hi, mid_, lo, hi, mid_, hi], axis=0).astype(jnp.bfloat16)
            hi, mid_, lo = pieces(row_v[...])
            col_v[...] = jnp.concatenate([hi, hi, hi, mid_, mid_, lo], axis=0).T.astype(jnp.bfloat16)
            turns()

            first = c == 0
            if first:
                for task in grams[0]:
                    task()
            both([bind(form_q, b) for b in range(nb)], grams[1] if first and nb > 1 else [])
            both(forms[0], (grams[2] if first and nb > 2 else []) + powers)
            for j in range(1, nb):
                both(forms[j], energies[j - 1])
            for task in energies[nb - 1]:
                task()
            power = jnp.sum(power_v[...], axis=1)
            energy = jnp.sum(level_v[:nb], axis=0, keepdims=True) + jnp.sum(energy_v[...], axis=1)
            energy = jnp.maximum(energy, power / snap_energy)
            energy = energy / receivers + 1e-06
            sum_v[c * span:(c + 1) * span, :] += power * (scale / snap_count) / (
                2.0 * receivers * energy)

    @pl.loop(0, freqs)
    def _(freq):
        for copy in loads(freq):
            copy.wait()
        count = counts[0, freq]
        for b in range(1, blocks + 1):
            low = count > (b - 1) * n
            cond = jnp.logical_and(low, count <= b * n) if b < blocks else low
            pl.when(cond)(functools.partial(run, freq, count, b))

    for r in range(ranges):
        out_ref[r] = sum_v[r:r + 1, :]


def partials(panels, snapshots, wavenumbers, mode_counts, mode_mask, mode_shapes, ranges, all_freqs):
    freqs, depths, modes = mode_shapes.shape
    receivers, snap_count = panels.shape[2], snapshots.shape[2]
    blocks, total_blocks = mode_mask.shape[1], mode_mask.shape[2]
    n = modes // blocks
    span = min(CHUNK, ranges)
    trig_rows = freqs * (ranges // span + 1)
    hbm = pl.BlockSpec(memory_space=pltpu.HBM)
    f32, bf16 = jnp.float32, jnp.bfloat16
    return pl.pallas_call(
        functools.partial(kernel, ranges=ranges, scale=1.0 / all_freqs),
        out_shape=jax.ShapeDtypeStruct((ranges, 1, depths), f32),
        in_specs=[hbm] * 6,
        out_specs=pl.BlockSpec(memory_space=pltpu.VMEM),
        scratch_shapes=[
            pltpu.SMEM((1, freqs), jnp.int32),
            pltpu.VMEM((freqs, depths, modes), bf16),
            pltpu.VMEM((freqs, 2, receivers, modes), bf16),
            pltpu.VMEM((freqs, 2, snap_count, receivers), bf16),
            pltpu.VMEM((freqs, modes), f32),
            pltpu.VMEM((blocks, freqs, total_blocks), jnp.int32),
            pltpu.VMEM((trig_rows, modes), f32),
            pltpu.VMEM((trig_rows, modes), f32),
            pltpu.VMEM((8, modes), f32),
            pltpu.VMEM((modes, 48), bf16),
            pltpu.VMEM((blocks, freqs, depths), f32),
            pltpu.VMEM((modes, depths), f32),
            pltpu.VMEM((modes + n, depths), bf16),
            pltpu.VMEM((2 * blocks, 2, n, n), f32),
            pltpu.VMEM((2, snap_count, modes), f32),
            pltpu.VMEM((span * n, 2 * n), bf16),
            pltpu.VMEM((span * n, 2 * n), bf16),
            pltpu.VMEM((span * n, 2 * n), bf16),
            pltpu.VMEM((span * 2 * snap_count, modes), bf16),
            pltpu.VMEM((8, depths), f32),
            pltpu.VMEM((span, 8, depths), f32),
            pltpu.VMEM((span, 8, depths), f32),
            pltpu.VMEM((ranges, depths), f32),
            pltpu.VMEM((5, 48, modes), bf16),
            pltpu.VMEM((2 * blocks, 5, n, n), f32),
            pltpu.SemaphoreType.DMA((5, freqs)),
        ],
        compiler_params=pltpu.CompilerParams(vmem_limit_bytes=24 << 20),
        name="bartlett",
    )(*(pltpu.with_memory_space_constraint(x, pltpu.HBM) for x in (
        mode_counts.reshape(1, -1), mode_shapes, panels, snapshots, wavenumbers,
        jnp.transpose(mode_mask, (1, 0, 2)))))


def on_device(panels, snapshots, wavenumbers, mode_counts, mode_mask, mode_shapes):
    freq_count = lax.axis_size("freq")
    tile_count = lax.axis_size("tile")
    depths = mode_shapes.shape[1]
    part = partials(
        panels, snapshots, wavenumbers, mode_counts, mode_mask, mode_shapes,
        tile_count * freq_count, panels.shape[0] * freq_count,
    )
    got = lax.all_to_all(part, ("tile", "freq"), 0, 0, tiled=True)
    return jnp.sum(got.reshape(tile_count, freq_count, depths), axis=1).reshape(1, -1)


def solution(mesh):
    in_specs = (
        P("freq", None, None, None),
        P(("groups", "freq"), None, None, None),
        P("freq", None),
        P("freq"),
        P("freq", None, None),
        P("freq", "tile", None),
    )
    out_specs = P(("groups", "tile", "freq"), None)
    return jax.shard_map(
        on_device, mesh=mesh, in_specs=in_specs, out_specs=out_specs, check_vma=False
    )
```

```python
import functools

import jax
import jax.numpy as jnp
from jax import lax
from jax.experimental import pallas as pl
from jax.experimental.pallas import tpu as pltpu
from jax.sharding import PartitionSpec as P

ZBLK = 32
ROWS = 16
HROWS = 32
PARTS = 2
CHUNK = 16
range_anchor = 1000.0
range_step = 25.0


def dot(a, b):
    return jnp.dot(a, b, preferred_element_type=jnp.float32)


def pieces(x):
    hi = x.astype(jnp.bfloat16).astype(jnp.float32)
    mid = (x - hi).astype(jnp.bfloat16).astype(jnp.float32)
    return hi, mid, x - hi - mid


def kernel(
    counts_hbm, shapes_hbm, panels_hbm, snaps_hbm, waves_hbm, mask_hbm, out_ref,
    counts, shapes_v, panels_v, snaps_v, waves_v, mask_v, cos_v, sin_v, row_v, col_v, live_v,
    phi_v, phib_v, gram_v, q_v, h0_v, h1_v, h2_v, w_v, level_v, energy_v, power_v, sum_v, pair_v, turn_v, sems,
    *, ranges, scale
):
    h_v = (h0_v, h1_v, h2_v)
    freqs, depths, modes = shapes_v.shape
    blocks = mask_v.shape[0]
    n = modes // blocks
    receivers = panels_v.shape[2]
    snap_count = snaps_v.shape[2]
    span = min(CHUNK, ranges)
    chunks = ranges // span
    mid = span // 2 - 1 if span > 1 else 0

    small = [
        pltpu.make_async_copy(waves_hbm, waves_v, sems.at[3, 0]),
        pltpu.make_async_copy(mask_hbm, mask_v, sems.at[4, 0]),
        pltpu.make_async_copy(counts_hbm, counts, sems.at[4, 1]),
    ]

    def loads(f):
        return [
            pltpu.make_async_copy(panels_hbm.at[f], panels_v.at[f], sems.at[0, f]),
            pltpu.make_async_copy(shapes_hbm.at[f], shapes_v.at[f], sems.at[1, f]),
            pltpu.make_async_copy(snaps_hbm.at[f], snaps_v.at[f], sems.at[2, f]),
        ]

    for copy in small:
        copy.start()
    for f in range(freqs):
        for copy in loads(f):
            copy.start()
    for copy in small:
        copy.wait()

    sum_v[...] = jnp.zeros_like(sum_v)
    waves = waves_v[...]
    angles = jnp.concatenate(
        [waves * range_step]
        + [waves * (range_anchor + range_step * (span * c + mid)) for c in range(chunks)], axis=0)
    cos_v[...] = jnp.cos(angles)
    sin_v[...] = jnp.sin(angles)
    first_block = lax.axis_index("tile") * (depths // ZBLK)
    total_blocks = mask_v.shape[2]
    pick = (
        lax.broadcasted_iota(jnp.int32, (total_blocks, depths), 0)
        == first_block + lax.broadcasted_iota(jnp.int32, (total_blocks, depths), 1) // ZBLK
    ).astype(jnp.bfloat16)
    for b in range(blocks):
        live_v[b] = dot(mask_v[b].astype(jnp.bfloat16), pick)

    def run(freq, count, nb):
        k = nb * n
        panel_re, panel_im = panels_v.at[freq, 0], panels_v.at[freq, 1]
        pairs = [(j, (j + 1) % nb if s else j) for j in range(nb) for s in range(2)]
        if nb == 1:
            pairs = [(0, 0)]
        elif nb == 2:
            pairs = [(0, 0), (0, 1), (1, 1)]
        width = [n * sum(1 for p in pairs if p[0] == j) for j in range(nb)]

        mode = lax.broadcasted_iota(jnp.int32, (n, 1), 0)
        for b in range(nb):
            part = shapes_v[freq, :, b * n:(b + 1) * n].T.astype(jnp.float32)
            part = part * live_v[b, pl.ds(freq, 1), :]
            part = jnp.where(mode + b * n < count, part, 0.0)
            phi_v[b * n:(b + 1) * n, :] = part
            phib_v[b * n:(b + 1) * n, :] = part.astype(jnp.bfloat16)
            if nb == 3 and b == 0:
                phib_v[3 * n:, :] = part.astype(jnp.bfloat16)

        snaps = jnp.concatenate([snaps_v[freq, 0], snaps_v[freq, 1]], axis=0)
        sp_re = dot(snaps, panel_re[:, :k])
        sp_im = dot(snaps, panel_im[:, :k])
        q_v[0, :, :k] = sp_re[:snap_count] + sp_im[snap_count:]
        q_v[1, :, :k] = sp_im[:snap_count] - sp_re[snap_count:]
        wide = snaps.astype(jnp.float32)
        snap_energy = jnp.maximum(jnp.sum(wide * wide, keepdims=True), 1e-30)

        eye = lax.broadcasted_iota(jnp.int32, (n, n), 0) == lax.broadcasted_iota(jnp.int32, (n, n), 1)

        lefts = [
            (panel_re[:, j * n:(j + 1) * n].T, panel_im[:, j * n:(j + 1) * n].T) for j in range(nb)]

        def gram(p):
            j, q = pairs[p]
            left_re, left_im = lefts[j]
            right_re = panel_re[:, q * n:(q + 1) * n]
            right_im = panel_im[:, q * n:(q + 1) * n]
            one = dot(
                jnp.concatenate([left_re, left_im], axis=1),
                jnp.concatenate([
                    jnp.concatenate([right_re, right_im], axis=1),
                    jnp.concatenate([right_im, -right_re], axis=1)], axis=0))
            g_re, g_im = one[:, :n], one[:, n:]
            if j == q:
                diag = jnp.sum(jnp.where(eye, g_re, 0.0), axis=1, keepdims=True)
                part = phi_v[j * n:(j + 1) * n, :]
                level_v[j:j + 1, :] = jnp.sum(part * part * diag, axis=0, keepdims=True)
                g_re = jnp.where(eye, 0.0, g_re)
                g_im = jnp.where(eye, 0.0, g_im)
            else:
                g_re, g_im = g_re * 2.0, g_im * 2.0
            gram_v[p, 0] = g_re
            gram_v[p, 1] = g_im

        def turns():
            for p, (j, q) in enumerate(pairs):
                right = jnp.concatenate([pair_v[x, :, q * n:(q + 1) * n] for x in range(5)], axis=1)
                both_of = dot(col_v[j * n:(j + 1) * n, :], right)
                for x in range(5):
                    turn_v[p, x] = both_of[:, x * n:(x + 1) * n]

        def form_q(b):
            at = slice(b * n, (b + 1) * n)
            zr, zi = q_v[0, :, at], q_v[1, :, at]
            c0, s0 = row_v[0:1, at], row_v[1:2, at]
            c1, s1 = row_v[2:3, at], row_v[3:4, at]
            turn = jnp.broadcast_to(2.0 * row_v[4:5, at], zr.shape)
            for row, low, high in (
                (0, zr * c0 - zi * s0, zr * c1 - zi * s1),
                (snap_count, zr * s0 + zi * c0, zr * s1 + zi * c1),
            ):
                a, z = low, high
                for r in range(mid, span):
                    lo = r * 2 * snap_count + row
                    w_v[lo:lo + snap_count, at] = a.astype(jnp.bfloat16)
                    if r + 1 < span:
                        a, z = z, turn * z - a
                a, z = turn * low - high, low
                for r in range(mid - 1, -1, -1):
                    lo = r * 2 * snap_count + row
                    w_v[lo:lo + snap_count, at] = a.astype(jnp.bfloat16)
                    if r:
                        a, z = turn * a - z, a

        def form_h(p, lo):
            j, q = pairs[p]
            slot = n * (p - [x[0] for x in pairs].index(j))
            g_re, g_im = gram_v[p, 0, lo:lo + HROWS, :], gram_v[p, 1, lo:lo + HROWS, :]

            cos0, sin0, cos1, sin1, turn = (
                turn_v[p, x, lo:lo + HROWS, :] for x in range(5))
            low, high = g_re * cos0 - g_im * sin0, g_re * cos1 - g_im * sin1
            h0, h1 = low, high
            for r in range(mid, span):
                h_v[j][r * n + lo:r * n + lo + HROWS, slot:slot + n] = h0.astype(jnp.bfloat16)
                if r + 1 < span:
                    h0, h1 = h1, turn * h1 - h0
            h0, h1 = turn * low - high, low
            for r in range(mid - 1, -1, -1):
                h_v[j][r * n + lo:r * n + lo + HROWS, slot:slot + n] = h0.astype(jnp.bfloat16)
                if r:
                    h0, h1 = turn * h0 - h1, h0

        step = span // PARTS if span % PARTS == 0 else span

        def power_of(c):
            y = dot(w_v[2 * snap_count * c:2 * snap_count * (c + step), :k], phib_v[:k, :])
            power_v[c:c + step] = jnp.sum((y * y).reshape(step, -1, 8, depths), axis=1)

        def energy_of(j, c):
            y = dot(h_v[j][n * c:n * (c + step), :width[j]], phib_v[j * n:j * n + width[j], :])
            y = y.reshape(step, n, depths) * phi_v[j * n:(j + 1) * n, :][None]
            y = jnp.sum(y.reshape(step, n // 8, 8, depths), axis=1)
            energy_v[c:c + step] = y if j == 0 else energy_v[c:c + step] + y

        def both(one, two):
            done = 0
            for i, task in enumerate(one):
                task()
                upto = (i + 1) * len(two) // len(one)
                for other in two[done:upto]:
                    other()
                done = upto
            for other in two[done:]:
                other()

        of = [[p for p in range(len(pairs)) if pairs[p][0] == j] for j in range(nb)]
        bind = functools.partial
        forms = [[bind(form_h, p, lo) for lo in range(0, n, HROWS) for p in of[j]] for j in range(nb)]
        grams = [[bind(gram, p) for p in of[j]] for j in range(nb)]
        starts = range(0, span, step)
        energies = [[bind(energy_of, j, c) for c in starts] for j in range(nb)]
        powers = [bind(power_of, c) for c in starts]

        for c in range(chunks):
            base = (c + 1) * freqs + freq
            cs, ss = cos_v[pl.ds(freq, 1), :], sin_v[pl.ds(freq, 1), :]
            c0, s0 = cos_v[pl.ds(base, 1), :], sin_v[pl.ds(base, 1), :]
            rows = [c0, s0, c0 * cs - s0 * ss, s0 * cs + c0 * ss, cs, ss, cs * 0.0, ss * 0.0]
            for i, row in enumerate(rows):
                row_v[i:i + 1, :] = row
            zero = jnp.zeros_like(c0)
            c1, s1 = rows[2], rows[3]
            for x, (at, one, two) in enumerate((
                (0, c0, s0), (0, s0, -c0), (2, c1, s1), (2, s1, -c1), (4, 2.0 * cs, 2.0 * ss))):
                spread = jnp.concatenate(
                    [one if i == at else two if i == at + 1 else zero for i in range(8)], axis=0)
                hi, mid_, lo = pieces(spread)
                pair_v[x] = jnp.concatenate([hi, mid_, lo, hi, mid_, hi], axis=0).astype(jnp.bfloat16)
            hi, mid_, lo = pieces(row_v[...])
            col_v[...] = jnp.concatenate([hi, hi, hi, mid_, mid_, lo], axis=0).T.astype(jnp.bfloat16)
            turns()

            first = c == 0
            if first:
                for task in grams[0]:
                    task()
            both([bind(form_q, b) for b in range(nb)], grams[1] if first and nb > 1 else [])
            both(forms[0], (grams[2] if first and nb > 2 else []) + powers)
            for j in range(1, nb):
                both(forms[j], energies[j - 1])
            for task in energies[nb - 1]:
                task()
            power = jnp.sum(power_v[...], axis=1)
            energy = jnp.sum(level_v[:nb], axis=0, keepdims=True) + jnp.sum(energy_v[...], axis=1)
            energy = jnp.maximum(energy, power / snap_energy)
            energy = energy / receivers + 1e-06
            sum_v[c * span:(c + 1) * span, :] += power * (scale / snap_count) / (
                2.0 * receivers * energy)

    @pl.loop(0, freqs)
    def _(freq):
        for copy in loads(freq):
            copy.wait()
        count = counts[0, freq]
        for b in range(1, blocks + 1):
            low = count > (b - 1) * n
            cond = jnp.logical_and(low, count <= b * n) if b < blocks else low
            pl.when(cond)(functools.partial(run, freq, count, b))

    for r in range(ranges):
        out_ref[r] = sum_v[r:r + 1, :]


def partials(panels, snapshots, wavenumbers, mode_counts, mode_mask, mode_shapes, ranges, all_freqs):
    freqs, depths, modes = mode_shapes.shape
    receivers, snap_count = panels.shape[2], snapshots.shape[2]
    blocks, total_blocks = mode_mask.shape[1], mode_mask.shape[2]
    n = modes // blocks
    span = min(CHUNK, ranges)
    trig_rows = freqs * (ranges // span + 1)
    hbm = pl.BlockSpec(memory_space=pltpu.HBM)
    f32, bf16 = jnp.float32, jnp.bfloat16
    return pl.pallas_call(
        functools.partial(kernel, ranges=ranges, scale=1.0 / all_freqs),
        out_shape=jax.ShapeDtypeStruct((ranges, 1, depths), f32),
        in_specs=[hbm] * 6,
        out_specs=pl.BlockSpec(memory_space=pltpu.VMEM),
        scratch_shapes=[
            pltpu.SMEM((1, freqs), jnp.int32),
            pltpu.VMEM((freqs, depths, modes), bf16),
            pltpu.VMEM((freqs, 2, receivers, modes), bf16),
            pltpu.VMEM((freqs, 2, snap_count, receivers), bf16),
            pltpu.VMEM((freqs, modes), f32),
            pltpu.VMEM((blocks, freqs, total_blocks), jnp.int32),
            pltpu.VMEM((trig_rows, modes), f32),
            pltpu.VMEM((trig_rows, modes), f32),
            pltpu.VMEM((8, modes), f32),
            pltpu.VMEM((modes, 48), bf16),
            pltpu.VMEM((blocks, freqs, depths), f32),
            pltpu.VMEM((modes, depths), f32),
            pltpu.VMEM((modes + n, depths), bf16),
            pltpu.VMEM((2 * blocks, 2, n, n), f32),
            pltpu.VMEM((2, snap_count, modes), f32),
            pltpu.VMEM((span * n, 2 * n), bf16),
            pltpu.VMEM((span * n, 2 * n), bf16),
            pltpu.VMEM((span * n, 2 * n), bf16),
            pltpu.VMEM((span * 2 * snap_count, modes), bf16),
            pltpu.VMEM((8, depths), f32),
            pltpu.VMEM((span, 8, depths), f32),
            pltpu.VMEM((span, 8, depths), f32),
            pltpu.VMEM((ranges, depths), f32),
            pltpu.VMEM((5, 48, modes), bf16),
            pltpu.VMEM((2 * blocks, 5, n, n), f32),
            pltpu.SemaphoreType.DMA((5, freqs)),
        ],
        compiler_params=pltpu.CompilerParams(vmem_limit_bytes=24 << 20),
        name="bartlett",
    )(*(pltpu.with_memory_space_constraint(x, pltpu.HBM) for x in (
        mode_counts.reshape(1, -1), mode_shapes, panels, snapshots, wavenumbers,
        jnp.transpose(mode_mask, (1, 0, 2)))))


def on_device(panels, snapshots, wavenumbers, mode_counts, mode_mask, mode_shapes):
    freq_count = lax.axis_size("freq")
    tile_count = lax.axis_size("tile")
    depths = mode_shapes.shape[1]
    part = partials(
        panels, snapshots, wavenumbers, mode_counts, mode_mask, mode_shapes,
        tile_count * freq_count, panels.shape[0] * freq_count,
    )
    got = lax.all_to_all(part, ("tile", "freq"), 0, 0, tiled=True)
    return jnp.sum(got.reshape(tile_count, freq_count, depths), axis=1).reshape(1, -1)


def solution(mesh):
    in_specs = (
        P("freq", None, None, None),
        P(("groups", "freq"), None, None, None),
        P("freq", None),
        P("freq"),
        P("freq", None, None),
        P("freq", "tile", None),
    )
    out_specs = P(("groups", "tile", "freq"), None)
    return jax.shard_map(
        on_device, mesh=mesh, in_specs=in_specs, out_specs=out_specs, check_vma=False
    )
```

```python
import functools

import jax
import jax.numpy as jnp
from jax import lax
from jax.experimental import pallas as pl
from jax.experimental.pallas import tpu as pltpu
from jax.sharding import PartitionSpec as P

ZBLK = 32
ROWS = 16
HROWS = 32
PARTS = 2
CHUNK = 16
range_anchor = 1000.0
range_step = 25.0


def dot(a, b):
    return jnp.dot(a, b, preferred_element_type=jnp.float32)


def pieces(x):
    hi = x.astype(jnp.bfloat16).astype(jnp.float32)
    mid = (x - hi).astype(jnp.bfloat16).astype(jnp.float32)
    return hi, mid, x - hi - mid


def kernel(
    counts_hbm, shapes_hbm, panels_hbm, snaps_hbm, waves_hbm, mask_hbm, out_ref,
    counts, shapes_v, panels_v, snaps_v, waves_v, mask_v, cos_v, sin_v, row_v, col_v, live_v,
    phi_v, phib_v, gram_v, q_v, h0_v, h1_v, h2_v, w_v, level_v, energy_v, power_v, sum_v, pair_v, turn_v, sems,
    *, ranges, last, scale
):
    h_v = (h0_v, h1_v, h2_v)
    freqs, depths, modes = shapes_v.shape
    blocks = mask_v.shape[0]
    n = modes // blocks
    receivers = panels_v.shape[2]
    snap_count = snaps_v.shape[2]
    span = min(CHUNK, ranges)
    chunks = ranges // span
    mid = span // 2 - 1 if span > 1 else 0

    small = [
        pltpu.make_async_copy(waves_hbm, waves_v, sems.at[3, 0]),
        pltpu.make_async_copy(mask_hbm, mask_v, sems.at[4, 0]),
        pltpu.make_async_copy(counts_hbm, counts, sems.at[4, 1]),
    ]

    def loads(f):
        return [
            pltpu.make_async_copy(panels_hbm.at[f], panels_v.at[f], sems.at[0, f]),
            pltpu.make_async_copy(shapes_hbm.at[f], shapes_v.at[f], sems.at[1, f]),
            pltpu.make_async_copy(snaps_hbm.at[f], snaps_v.at[f], sems.at[2, f]),
        ]

    for copy in small:
        copy.start()
    for f in range(freqs):
        for copy in loads(f):
            copy.start()
    for copy in small:
        copy.wait()

    sum_v[...] = jnp.zeros_like(sum_v)
    waves = waves_v[...]
    angles = jnp.concatenate(
        [waves * range_step]
        + [waves * (range_anchor + range_step * (span * c + mid)) for c in range(chunks)], axis=0)
    cos_v[...] = jnp.cos(angles)
    sin_v[...] = jnp.sin(angles)
    first_block = lax.axis_index("tile") * (depths // ZBLK)
    total_blocks = mask_v.shape[2]
    pick = (
        lax.broadcasted_iota(jnp.int32, (total_blocks, depths), 0)
        == first_block + lax.broadcasted_iota(jnp.int32, (total_blocks, depths), 1) // ZBLK
    ).astype(jnp.bfloat16)
    for b in range(blocks):
        live_v[b] = dot(mask_v[b].astype(jnp.bfloat16), pick)

    def run(freq, count, nb):
        k = nb * n
        panel_re, panel_im = panels_v.at[freq, 0], panels_v.at[freq, 1]
        pairs = [(j, (j + 1) % nb if s else j) for j in range(nb) for s in range(2)]
        if nb == 1:
            pairs = [(0, 0)]
        elif nb == 2:
            pairs = [(0, 0), (0, 1), (1, 1)]
        width = [n * sum(1 for p in pairs if p[0] == j) for j in range(nb)]

        mode = lax.broadcasted_iota(jnp.int32, (n, 1), 0)
        for b in range(nb):
            part = shapes_v[freq, :, b * n:(b + 1) * n].T.astype(jnp.float32)
            part = part * live_v[b, pl.ds(freq, 1), :]
            part = jnp.where(mode + b * n < count, part, 0.0)
            phi_v[b * n:(b + 1) * n, :] = part
            phib_v[b * n:(b + 1) * n, :] = part.astype(jnp.bfloat16)
            if nb == 3 and b == 0:
                phib_v[3 * n:, :] = part.astype(jnp.bfloat16)

        snaps = jnp.concatenate([snaps_v[freq, 0], snaps_v[freq, 1]], axis=0)
        sp_re = dot(snaps, panel_re[:, :k])
        sp_im = dot(snaps, panel_im[:, :k])
        q_v[0, :, :k] = sp_re[:snap_count] + sp_im[snap_count:]
        q_v[1, :, :k] = sp_im[:snap_count] - sp_re[snap_count:]
        wide = snaps.astype(jnp.float32)
        snap_energy = jnp.maximum(jnp.sum(wide * wide, keepdims=True), 1e-30)

        eye = lax.broadcasted_iota(jnp.int32, (n, n), 0) == lax.broadcasted_iota(jnp.int32, (n, n), 1)

        lefts = [
            (panel_re[:, j * n:(j + 1) * n].T, panel_im[:, j * n:(j + 1) * n].T) for j in range(nb)]

        def gram(p):
            j, q = pairs[p]
            left_re, left_im = lefts[j]
            right_re = panel_re[:, q * n:(q + 1) * n]
            right_im = panel_im[:, q * n:(q + 1) * n]
            one = dot(
                jnp.concatenate([left_re, left_im], axis=1),
                jnp.concatenate([
                    jnp.concatenate([right_re, right_im], axis=1),
                    jnp.concatenate([right_im, -right_re], axis=1)], axis=0))
            g_re, g_im = one[:, :n], one[:, n:]
            if j == q:
                diag = jnp.sum(jnp.where(eye, g_re, 0.0), axis=1, keepdims=True)
                part = phi_v[j * n:(j + 1) * n, :]
                level_v[j:j + 1, :] = jnp.sum(part * part * diag, axis=0, keepdims=True)
                g_re = jnp.where(eye, 0.0, g_re)
                g_im = jnp.where(eye, 0.0, g_im)
            else:
                g_re, g_im = g_re * 2.0, g_im * 2.0
            gram_v[p, 0] = g_re
            gram_v[p, 1] = g_im

        def turns():
            for p, (j, q) in enumerate(pairs):
                right = jnp.concatenate([pair_v[x, :, q * n:(q + 1) * n] for x in range(5)], axis=1)
                both_of = dot(col_v[j * n:(j + 1) * n, :], right)
                for x in range(5):
                    turn_v[p, x] = both_of[:, x * n:(x + 1) * n]

        def form_q(b):
            at = slice(b * n, (b + 1) * n)
            zr, zi = q_v[0, :, at], q_v[1, :, at]
            c0, s0 = row_v[0:1, at], row_v[1:2, at]
            c1, s1 = row_v[2:3, at], row_v[3:4, at]
            turn = jnp.broadcast_to(2.0 * row_v[4:5, at], zr.shape)
            for row, low, high in (
                (0, zr * c0 - zi * s0, zr * c1 - zi * s1),
                (snap_count, zr * s0 + zi * c0, zr * s1 + zi * c1),
            ):
                a, z = low, high
                for r in range(mid, span):
                    lo = r * 2 * snap_count + row
                    w_v[lo:lo + snap_count, at] = a.astype(jnp.bfloat16)
                    if r + 1 < span:
                        a, z = z, turn * z - a
                a, z = turn * low - high, low
                for r in range(mid - 1, -1, -1):
                    lo = r * 2 * snap_count + row
                    w_v[lo:lo + snap_count, at] = a.astype(jnp.bfloat16)
                    if r:
                        a, z = turn * a - z, a

        def form_h(p, lo):
            j, q = pairs[p]
            slot = n * (p - [x[0] for x in pairs].index(j))
            g_re, g_im = gram_v[p, 0, lo:lo + HROWS, :], gram_v[p, 1, lo:lo + HROWS, :]

            cos0, sin0, cos1, sin1, turn = (
                turn_v[p, x, lo:lo + HROWS, :] for x in range(5))
            low, high = g_re * cos0 - g_im * sin0, g_re * cos1 - g_im * sin1
            h0, h1 = low, high
            for r in range(mid, span):
                h_v[j][r * n + lo:r * n + lo + HROWS, slot:slot + n] = h0.astype(jnp.bfloat16)
                if r + 1 < span:
                    h0, h1 = h1, turn * h1 - h0
            h0, h1 = turn * low - high, low
            for r in range(mid - 1, -1, -1):
                h_v[j][r * n + lo:r * n + lo + HROWS, slot:slot + n] = h0.astype(jnp.bfloat16)
                if r:
                    h0, h1 = turn * h0 - h1, h0

        step = span // PARTS if span % PARTS == 0 else span

        def power_of(c):
            y = dot(w_v[2 * snap_count * c:2 * snap_count * (c + step), :k], phib_v[:k, :])
            power_v[c:c + step] = jnp.sum((y * y).reshape(step, -1, 8, depths), axis=1)

        def energy_of(j, c):
            y = dot(h_v[j][n * c:n * (c + step), :width[j]], phib_v[j * n:j * n + width[j], :])
            y = y.reshape(step, n, depths) * phi_v[j * n:(j + 1) * n, :][None]
            y = jnp.sum(y.reshape(step, n // 8, 8, depths), axis=1)
            energy_v[c:c + step] = y if j == 0 else energy_v[c:c + step] + y

        def both(one, two):
            done = 0
            for i, task in enumerate(one):
                task()
                upto = (i + 1) * len(two) // len(one)
                for other in two[done:upto]:
                    other()
                done = upto
            for other in two[done:]:
                other()

        of = [[p for p in range(len(pairs)) if pairs[p][0] == j] for j in range(nb)]
        bind = functools.partial
        forms = [[bind(form_h, p, lo) for lo in range(0, n, HROWS) for p in of[j]] for j in range(nb)]
        grams = [[bind(gram, p) for p in of[j]] for j in range(nb)]
        starts = range(0, span, step)
        energies = [[bind(energy_of, j, c) for c in starts] for j in range(nb)]
        powers = [bind(power_of, c) for c in starts]

        for c in range(chunks):
            base = (c + 1) * freqs + freq
            cs, ss = cos_v[pl.ds(freq, 1), :], sin_v[pl.ds(freq, 1), :]
            c0, s0 = cos_v[pl.ds(base, 1), :], sin_v[pl.ds(base, 1), :]
            rows = [c0, s0, c0 * cs - s0 * ss, s0 * cs + c0 * ss, cs, ss, cs * 0.0, ss * 0.0]
            for i, row in enumerate(rows):
                row_v[i:i + 1, :] = row
            zero = jnp.zeros_like(c0)
            c1, s1 = rows[2], rows[3]
            for x, (at, one, two) in enumerate((
                (0, c0, s0), (0, s0, -c0), (2, c1, s1), (2, s1, -c1), (4, 2.0 * cs, 2.0 * ss))):
                spread = jnp.concatenate(
                    [one if i == at else two if i == at + 1 else zero for i in range(8)], axis=0)
                hi, mid_, lo = pieces(spread)
                pair_v[x] = jnp.concatenate([hi, mid_, lo, hi, mid_, hi], axis=0).astype(jnp.bfloat16)
            hi, mid_, lo = pieces(row_v[...])
            col_v[...] = jnp.concatenate([hi, hi, hi, mid_, mid_, lo], axis=0).T.astype(jnp.bfloat16)
            turns()

            first = c == 0
            if first:
                for task in grams[0]:
                    task()
            both([bind(form_q, b) for b in range(nb)], grams[1] if first and nb > 1 else [])
            both(forms[0], (grams[2] if first and nb > 2 else []) + powers)
            for j in range(1, nb):
                both(forms[j], energies[j - 1])
            for task in energies[nb - 1]:
                task()
            power = jnp.sum(power_v[...], axis=1)
            energy = jnp.sum(level_v[:nb], axis=0, keepdims=True) + jnp.sum(energy_v[...], axis=1)
            energy = jnp.maximum(energy, power / snap_energy)
            energy = energy / receivers + 1e-06
            sum_v[c * span:(c + 1) * span, :] += power * (scale / snap_count) / (
                2.0 * receivers * energy)

    @pl.loop(0, freqs)
    def _(freq):
        for copy in loads(freq):
            copy.wait()
        count = counts[0, freq]
        for b in range(1, blocks + 1):
            low = count > (b - 1) * n
            cond = jnp.logical_and(low, count <= b * n) if b < blocks else low
            pl.when(cond)(functools.partial(run, freq, count, b))

    for r in range(ranges):
        out_ref[r % last * (ranges // last) + r // last] = sum_v[r:r + 1, :]


def partials(panels, snapshots, wavenumbers, mode_counts, mode_mask, mode_shapes, ranges, last, all_freqs):
    freqs, depths, modes = mode_shapes.shape
    receivers, snap_count = panels.shape[2], snapshots.shape[2]
    blocks, total_blocks = mode_mask.shape[1], mode_mask.shape[2]
    n = modes // blocks
    span = min(CHUNK, ranges)
    trig_rows = freqs * (ranges // span + 1)
    hbm = pl.BlockSpec(memory_space=pltpu.HBM)
    f32, bf16 = jnp.float32, jnp.bfloat16
    return pl.pallas_call(
        functools.partial(kernel, ranges=ranges, last=last, scale=1.0 / all_freqs),
        out_shape=jax.ShapeDtypeStruct((ranges, 1, depths), f32),
        in_specs=[hbm] * 6,
        out_specs=pl.BlockSpec(memory_space=pltpu.VMEM),
        scratch_shapes=[
            pltpu.SMEM((1, freqs), jnp.int32),
            pltpu.VMEM((freqs, depths, modes), bf16),
            pltpu.VMEM((freqs, 2, receivers, modes), bf16),
            pltpu.VMEM((freqs, 2, snap_count, receivers), bf16),
            pltpu.VMEM((freqs, modes), f32),
            pltpu.VMEM((blocks, freqs, total_blocks), jnp.int32),
            pltpu.VMEM((trig_rows, modes), f32),
            pltpu.VMEM((trig_rows, modes), f32),
            pltpu.VMEM((8, modes), f32),
            pltpu.VMEM((modes, 48), bf16),
            pltpu.VMEM((blocks, freqs, depths), f32),
            pltpu.VMEM((modes, depths), f32),
            pltpu.VMEM((modes + n, depths), bf16),
            pltpu.VMEM((2 * blocks, 2, n, n), f32),
            pltpu.VMEM((2, snap_count, modes), f32),
            pltpu.VMEM((span * n, 2 * n), bf16),
            pltpu.VMEM((span * n, 2 * n), bf16),
            pltpu.VMEM((span * n, 2 * n), bf16),
            pltpu.VMEM((span * 2 * snap_count, modes), bf16),
            pltpu.VMEM((8, depths), f32),
            pltpu.VMEM((span, 8, depths), f32),
            pltpu.VMEM((span, 8, depths), f32),
            pltpu.VMEM((ranges, depths), f32),
            pltpu.VMEM((5, 48, modes), bf16),
            pltpu.VMEM((2 * blocks, 5, n, n), f32),
            pltpu.SemaphoreType.DMA((5, freqs)),
        ],
        compiler_params=pltpu.CompilerParams(vmem_limit_bytes=24 << 20),
        name="bartlett",
    )(*(pltpu.with_memory_space_constraint(x, pltpu.HBM) for x in (
        mode_counts.reshape(1, -1), mode_shapes, panels, snapshots, wavenumbers,
        jnp.transpose(mode_mask, (1, 0, 2)))))


def on_device(panels, snapshots, wavenumbers, mode_counts, mode_mask, mode_shapes):
    freq_count = lax.axis_size("freq")
    tile_count = lax.axis_size("tile")
    depths = mode_shapes.shape[1]
    part = partials(
        panels, snapshots, wavenumbers, mode_counts, mode_mask, mode_shapes,
        tile_count * freq_count, freq_count, panels.shape[0] * freq_count,
    )
    got = lax.all_to_all(part, ("freq", "tile"), 0, 0, tiled=True)
    return sum(got[f * tile_count:(f + 1) * tile_count] for f in range(freq_count)).reshape(1, -1)


def solution(mesh):
    in_specs = (
        P("freq", None, None, None),
        P(("groups", "freq"), None, None, None),
        P("freq", None),
        P("freq"),
        P("freq", None, None),
        P("freq", "tile", None),
    )
    out_specs = P(("groups", "tile", "freq"), None)
    return jax.shard_map(
        on_device, mesh=mesh, in_specs=in_specs, out_specs=out_specs, check_vma=False
    )
```
